32 devices in a mesh: struct: 4 (over y, x), fluid: 8 (over z, core).
Axes of the slice: x: 2, y: 2, z: 4, core: 2. Of those that a mesh axis runs over, the one named last changes fastest.
Arguments:
- shell_motion: float32 [3, 262144], P(None, ('struct', 'fluid')), may hold values from -6 to 6
- owner: int32 [262144, 1], P(('struct', 'fluid')), may hold values from 0 to 31; in each aligned block of 8192 rows (0 to 8191, 8192 to 16383, ...) at most 512 rows name the same one
- stencil_slot: int32 [4, 8, 64, 128], P(None, 'struct', 'fluid'), may hold values from 0 to 16383
- stencil_weight: float32 [4, 8, 64, 128], P(None, 'struct', 'fluid'), may hold values from 0 to 0.5
- prev_motion: float32 [3, 8, 64, 256], P(None, 'struct', 'fluid'), may hold values from -6 to 6
- node_offset: float32 [3, 8, 64, 256], P(None, 'struct', 'fluid'), may hold values from -0.07 to 0.07
- cell_split: int32 [8, 64, 256], P('struct', 'fluid'), may hold values from 0 to 3
Outputs:
- mesh_motion: float32 [3, 8, 64, 256], P(None, 'struct', 'fluid')
The draws below stay inside these ranges and needn't reach their ends.
Inputs may be any that keep to these rules, and one draw needn't show every extreme that they name: Among the 8192 shell nodes of one device, no owner is named by more than 512 of them, a bound that some block reaches.
All inputs are finite; a program needn't handle non-finite values.
Results may differ from the reference program's by a relative error of at most 0.0003.
Values sent between devices are 32-bit elements; how exact they have to be, the bound alone decides.
A program may use at most 64 MiB of HBM per device.

```python
import math
from functools import partial
from functools import reduce
import jax
import jax.numpy as jnp
import numpy as np
from jax import lax

CY = 2
CZ = 8
NX = 256
IF_DEV = 8192
WALL = 128
STENCIL = 4
SWEEPS = 4
NY = 8
NZ = 64
NIF = 262144
CAP = 512
SLOTS = 16384
N_STRUCT = 4
N_FLUID = 8
DEVICES = 32


def with_ends(values, key, smallest, high):
    extent = values.shape
    place = [jax.random.randint(jax.random.fold_in(key, axis), (), 0, extent[axis]) for axis in range(len(extent))]
    values = values.at[tuple(place)].set(smallest)
    longest = extent.index(max(extent))
    place[longest] = (place[longest] + 1) % extent[longest]
    return values.at[tuple(place)].set(high)


def shard_levels(own_key, extent, shards, smallest, largest):
    def one(axis_at, blocks):
        heights = jax.random.uniform(jax.random.fold_in(jax.random.fold_in(own_key, 6), axis_at), (blocks,), jnp.float32, smallest / len(shards), largest / len(shards))
        return jnp.repeat(jnp.exp(heights), extent[axis_at] // blocks).reshape((-1,) + (1,) * (len(extent) - axis_at - 1))

    factor_of = one(*shards[0])
    for cut in shards[1:]:
        factor_of = factor_of * one(*cut)
    return factor_of


def deal_out(key, own, number, rows, amount, top, reach, lean):
    ranking = jax.random.permutation(key, amount)
    heavy_load, usual = load_shares(amount, rows * top, reach, lean, True), load_shares(amount, rows * top, reach, lean, False)
    places = jnp.arange(amount)

    def named(sizes, turn):
        used = int((sizes > 0).sum())
        fixed = max(1, used // 4)
        passed = fixed + (places - fixed + turn * (used - fixed)) % max(1, amount - fixed)
        return jnp.zeros((amount,), jnp.int32).at[ranking[jnp.where(places < fixed, places, passed)]].set(jnp.asarray(sizes, jnp.int32))

    sizes = jnp.where(number % 4 == 0, named(heavy_load, number // 4), named(usual, number - number // 4 - 1))
    mixed = jax.random.permutation(jax.random.fold_in(own, 3), amount)
    giver, receiver = mixed[0:amount // 2 * 2:2], mixed[1:amount // 2 * 2:2]
    room = jnp.minimum(sizes[giver] - 1, reach - sizes[receiver]) // 2
    room = jnp.where((giver == ranking[0]) | (receiver == ranking[0]) | (sizes[receiver] == 0), 0, jnp.maximum(room, 0))
    passed = jax.random.randint(jax.random.fold_in(own, 4), (amount // 2,), 0, 1 << 20) % (room + 1)
    sizes = sizes.at[giver].add(-passed).at[receiver].add(passed)
    items = jnp.searchsorted(jnp.cumsum(sizes), jnp.arange(rows * top), side="right").astype(jnp.int32)
    table = items.reshape(top, rows).T
    table = table[jax.random.permutation(jax.random.fold_in(own, 1), rows)]
    turn = jax.random.randint(jax.random.fold_in(own, 2), (rows, 1), 0, top)
    return jnp.take_along_axis(table, (jnp.arange(top)[None, :] + turn) % top, axis=1)


def load_shares(count, total, limit, slope, full):
    loads = [(1 << 20) // math.isqrt(standing ** slope) + 1 for standing in range(1, count + 1)]
    largest = limit if full else min(limit, max(-(-total // count), total * loads[0] // sum(loads)))
    least = 1 if total - largest >= count - 1 else 0
    given, surplus = [largest] + [least] * (count - 1), total - largest - least * (count - 1)
    while surplus > 0:
        free = [i for i in range(1, count) if given[i] < largest] or [i for i in range(1, count) if given[i] < limit]
        pool, left = sum([loads[i] for i in free]), surplus
        for i in free:
            more = min(limit - given[i], max(1, left * loads[i] // pool), surplus)
            given[i] = given[i] + more
            surplus = surplus - more
    return np.array(given)


def normal_values(stream_key, dims, deviation, most, cuts=(), kind=jnp.bfloat16):
    gain = shard_levels(stream_key, dims, cuts, -0.22, 0.18) if cuts else 1.0
    array = jax.random.normal(stream_key, dims, jnp.float32) * deviation * gain
    return jnp.minimum(jnp.maximum(array, -most), most).astype(kind)


def setup_inputs(seed: int = 0) -> dict:
    key_of = jax.random.split(jax.random.key(seed), 8)
    shell_motion = normal_values(key_of[0], (3, NIF), 1.0, 6.0, ((1, 32),), jnp.float32)
    owner_keys = jax.random.split(jax.random.fold_in(key_of[1], 1), NIF // IF_DEV)
    owner_turns = jax.random.permutation(jax.random.fold_in(key_of[1], 3), NIF // IF_DEV)
    owner = jax.vmap(lambda own, number: deal_out(jax.random.fold_in(key_of[1], 2), own, number, IF_DEV, DEVICES, 1, CAP, 2))(owner_keys, owner_turns).reshape((NIF, 1))
    stencil_slot = with_ends(jax.random.randint(key_of[2], (STENCIL, NY, NZ, WALL), 0, SLOTS), jax.random.fold_in(key_of[2], 1), 0, SLOTS - 1).astype(jnp.int32)
    stencil_weight = jnp.clip(0.5 * jax.random.uniform(key_of[3], (STENCIL, NY, NZ, WALL), jnp.float32) ** shard_levels(key_of[3], (STENCIL, NY, NZ, WALL), ((1, 4), (2, 8)), -0.2, 0.2), 0.0, 0.5)
    prev_motion = normal_values(key_of[4], (3, NY, NZ, NX), 1.0, 6.0, ((1, 4), (2, 8)), jnp.float32)
    node_offset = jnp.clip(jax.random.uniform(key_of[5], (3, NY, NZ, NX), jnp.float32, -0.07, 0.07) * shard_levels(key_of[5], (3, NY, NZ, NX), ((1, 4), (2, 8)), -0.4, 0.0), -0.07, 0.07)
    cell_split = with_ends(jax.random.randint(key_of[6], (NY, NZ, NX), 0, 4), jax.random.fold_in(key_of[6], 1), 0, 3).astype(jnp.int32)
    return dict(shell_motion=shell_motion, owner=owner, stencil_slot=stencil_slot, stencil_weight=stencil_weight, prev_motion=prev_motion, node_offset=node_offset, cell_split=cell_split)


LAMBDA_RATIO = 1.0
RELAX_FACTOR = 0.5
STEP_ORDERS = ((0, 1, 2), (0, 2, 1), (1, 0, 2), (1, 2, 0), (2, 0, 1), (2, 1, 0))
CORNER_LIST = tuple((shift_x, shift_y, shift_z) for shift_x in (0, 1) for shift_y in (0, 1) for shift_z in (0, 1))


def cross_product(left_vec, right_vec):
    return jnp.stack([left_vec[1] * right_vec[2] - left_vec[2] * right_vec[1],
                      left_vec[2] * right_vec[0] - left_vec[0] * right_vec[2],
                      left_vec[0] * right_vec[1] - left_vec[1] * right_vec[0]])


def select_flip(flip_y, flip_z, unflipped, flipped_z, flipped_y, flipped_both):
    return jnp.where(flip_y, jnp.where(flip_z, flipped_both, flipped_y), jnp.where(flip_z, flipped_z, unflipped))


def reflect_corners(corners, flip_y, flip_z):
    result = {}
    for corner in CORNER_LIST:
        shift_x, shift_y, shift_z = corner
        result[corner] = select_flip(flip_y, flip_z, corners[corner], corners[(shift_x, shift_y, 1 - shift_z)],
                                     corners[(shift_x, 1 - shift_y, shift_z)], corners[(shift_x, 1 - shift_y, 1 - shift_z)])
    return result


def flip_masks(split_codes):
    flip_y = (split_codes // 2) == 1
    flip_z = (split_codes % 2) == 1
    sign_y = jnp.where(flip_y, -1.0, 1.0).astype(jnp.float32)
    sign_z = jnp.where(flip_z, -1.0, 1.0).astype(jnp.float32)
    return flip_y, flip_z, sign_y, sign_z


def lattice_edge(vertex, sign_y, sign_z):
    return jnp.stack([jnp.full_like(sign_y, float(vertex[0])), sign_y * vertex[1], sign_z * vertex[2]])


def element_gradients(offsets, step_order, sign_y, sign_z):
    position = [0, 0, 0]
    vertex_path = [(0, 0, 0)]
    for axis_id in step_order:
        position[axis_id] = 1
        vertex_path.append(tuple(position))
    anchor = offsets[vertex_path[0]]
    edge_list = [lattice_edge(vertex, sign_y, sign_z) + offsets[vertex] - anchor for vertex in vertex_path[1:]]
    across_one = cross_product(edge_list[1], edge_list[2])
    across_two = cross_product(edge_list[2], edge_list[0])
    across_three = cross_product(edge_list[0], edge_list[1])
    volume_six = jnp.sum(edge_list[0] * across_one, axis=0)
    grad_one = across_one / volume_six
    grad_two = across_two / volume_six
    grad_three = across_three / volume_six
    grad_zero = -(grad_one + grad_two + grad_three)
    return vertex_path, [grad_zero, grad_one, grad_two, grad_three]


def element_forces(offsets, displace, sign_y, sign_z):
    forces = {corner: jnp.zeros_like(displace[corner]) for corner in CORNER_LIST}
    for step_order in STEP_ORDERS:
        vertex_path, gradient_list = element_gradients(offsets, step_order, sign_y, sign_z)
        tensor = displace[vertex_path[0]][:, None] * gradient_list[0][None, :]
        for vertex in range(1, 4):
            tensor = tensor + displace[vertex_path[vertex]][:, None] * gradient_list[vertex][None, :]
        trace_sum = tensor[0, 0] + tensor[1, 1] + tensor[2, 2]
        symmetric = tensor + jnp.swapaxes(tensor, 0, 1)
        for vertex in range(4):
            gradient = gradient_list[vertex]
            nodal_force = LAMBDA_RATIO * trace_sum * gradient + jnp.sum(symmetric * gradient[None, :], axis=1)
            forces[vertex_path[vertex]] = forces[vertex_path[vertex]] + nodal_force
    return forces


def element_diagonal(offsets, sign_y, sign_z):
    result = {corner: jnp.zeros_like(offsets[corner]) for corner in CORNER_LIST}
    for step_order in STEP_ORDERS:
        vertex_path, gradient_list = element_gradients(offsets, step_order, sign_y, sign_z)
        for vertex in range(4):
            gradient = gradient_list[vertex]
            entry = (LAMBDA_RATIO + 1.0) * gradient * gradient + jnp.sum(gradient * gradient, axis=0)
            result[vertex_path[vertex]] = result[vertex_path[vertex]] + entry
    return result


def row_corners(lower, upper):
    return {corner: jnp.roll(upper if corner[1] else lower, (-corner[2], -corner[0]), axis=(-2, -1)) for corner in CORNER_LIST}


def row_assemble(per_corner):
    lower_part = reduce(jnp.add, [jnp.roll(per_corner[corner], (corner[2], corner[0]), axis=(-2, -1)) for corner in CORNER_LIST if corner[1] == 0])
    upper_part = reduce(jnp.add, [jnp.roll(per_corner[corner], (corner[2], corner[0]), axis=(-2, -1)) for corner in CORNER_LIST if corner[1] == 1])
    return lower_part, upper_part


def combine_rows(pair):
    lower_part, upper_part = pair
    return jnp.transpose(lower_part + jnp.roll(upper_part, 1, axis=0), (1, 0, 2, 3))


def row_slices(nodal_field, row_index):
    lower = lax.dynamic_index_in_dim(nodal_field, row_index, 1, keepdims=False)
    upper = lax.dynamic_index_in_dim(nodal_field, (row_index + 1) % NY, 1, keepdims=False)
    return row_corners(lower, upper)


def row_masks(cell_split, row_index):
    return flip_masks(lax.dynamic_index_in_dim(cell_split, row_index, 0, keepdims=False))


def diagonal_row(node_offset, cell_split, row_index):
    flip_y, flip_z, sign_y, sign_z = row_masks(cell_split, row_index)
    offsets = reflect_corners(row_slices(node_offset, row_index), flip_y, flip_z)
    return row_assemble(reflect_corners(element_diagonal(offsets, sign_y, sign_z), flip_y, flip_z))


def force_row(node_offset, cell_split, current, row_index):
    flip_y, flip_z, sign_y, sign_z = row_masks(cell_split, row_index)
    offsets = reflect_corners(row_slices(node_offset, row_index), flip_y, flip_z)
    displace = reflect_corners(row_slices(current, row_index), flip_y, flip_z)
    return row_assemble(reflect_corners(element_forces(offsets, displace, sign_y, sign_z), flip_y, flip_z))


def reference(shell_motion, owner, stencil_slot, stencil_weight, prev_motion, node_offset, cell_split):
    devices = N_STRUCT * N_FLUID
    slot_count = devices * CAP
    targets = jnp.arange(devices, dtype=jnp.int32)

    def pack_source(source):
        owner_rows = lax.dynamic_slice_in_dim(owner[:, 0], source * IF_DEV, IF_DEV)
        values = lax.dynamic_slice_in_dim(shell_motion, source * IF_DEV, IF_DEV, 1)
        onehot = (owner_rows[:, None] == targets[None, :]).astype(jnp.int32)
        before = jnp.cumsum(onehot, axis=0) - onehot
        slot_rank = jnp.sum(before * onehot, axis=1)
        slot_place = (owner_rows * CAP + slot_rank).astype(jnp.int32)
        return jnp.zeros((3, slot_count), dtype=shell_motion.dtype).at[:, slot_place].set(values)

    packed = lax.map(pack_source, targets)
    received = packed.reshape(devices, 3, devices, CAP).transpose(1, 2, 0, 3).reshape(3, devices * slot_count)
    row_owner = (jnp.arange(NY, dtype=jnp.int32) // CY) * N_FLUID
    column_owner = jnp.arange(NZ, dtype=jnp.int32) // CZ
    holder = row_owner[:, None] + column_owner[None, :]
    flat_index = (holder[None, :, :, None] * slot_count + stencil_slot).astype(jnp.int32)
    gathered = jnp.take(received, flat_index.reshape(-1), axis=1).reshape(3, STENCIL, NY, NZ, WALL)
    wall_values = jnp.sum(stencil_weight[None] * gathered, axis=1)
    motion = jnp.concatenate([wall_values, prev_motion[:, :, :, WALL:]], axis=3)
    is_wall = (jnp.arange(NX, dtype=jnp.int32) < WALL)[None, None, None, :]
    rows_index = jnp.arange(NY, dtype=jnp.int32)
    diagonal = combine_rows(lax.map(partial(diagonal_row, node_offset, cell_split), rows_index))
    for sweep_index in range(SWEEPS):
        forces = combine_rows(lax.map(partial(force_row, node_offset, cell_split, motion), rows_index))
        motion = jnp.where(is_wall, motion, motion - RELAX_FACTOR * forces / diagonal)
    return motion
```

```python
import functools

import jax
import jax.numpy as jnp
from jax import lax
from jax.experimental import pallas as pl
from jax.experimental.pallas import tpu as pltpu
from jax.sharding import PartitionSpec as P

SWEEPS = 4
LANES = 128
LAMBDA_RATIO = 1.0
RELAX_FACTOR = 0.5
STEP_ORDERS = ((0, 1, 2), (0, 2, 1), (1, 0, 2), (1, 2, 0), (2, 0, 1), (2, 1, 0))
CORNERS = tuple((a, b, c) for a in (0, 1) for b in (0, 1) for c in (0, 1))
BF16 = jnp.bfloat16
F32 = jnp.float32


def from_behind(block, axis, distance):
    count = lax.axis_size(axis)
    route = [((i - distance) % count, i) for i in range(count)]
    return lax.ppermute(block, axis, route)


def widen(block, axis, dim, depth):
    count, size = lax.axis_size(axis), block.shape[dim]
    whole = {0: block}

    def part(distance, low, high):
        key = distance % count
        if high - low < size and key != 0:
            return from_behind(lax.slice_in_dim(block, low, high, axis=dim), axis, distance)
        if key not in whole:
            whole[key] = from_behind(block, axis, distance)
        return lax.slice_in_dim(whole[key], low, high, axis=dim)

    below, above, left = [], [], depth
    distance = 1
    while left > 0:
        taken = min(left, size)
        below.insert(0, part(distance, size - taken, size))
        above.append(part(-distance, 0, taken))
        left -= taken
        distance += 1
    return jnp.concatenate(below + [block] + above, axis=dim)


def split_two(values):
    high = values.astype(BF16)
    low = (values - high.astype(F32)).astype(BF16)
    return high, low


def iota(shape, dim):
    return lax.broadcasted_iota(jnp.int32, shape, dim)


def pack_kernel(devices, capacity, own_ref, val_ref, out_ref, place_ref, acc_ref):
    rows = own_ref.shape[0]
    wide = 2 * LANES
    groups = devices * capacity // wide
    own = own_ref[...]
    upper = (iota((LANES, LANES), 0) < iota((LANES, LANES), 1)).astype(F32)
    prefix_all = jnp.concatenate([upper, jnp.ones((LANES, LANES), F32)], axis=1).astype(BF16)
    lower = (iota((rows, rows), 1) < iota((rows, rows), 0)).astype(F32).astype(BF16)
    chunk = min(devices, 32)

    def ranks(step, place):
        for o in range(chunk):
            target = step * chunk + o
            named = own == target
            both = jnp.dot(named.astype(F32).astype(BF16), prefix_all, preferred_element_type=F32)
            ahead = jnp.dot(lower, both[:, LANES:].astype(BF16), preferred_element_type=F32)
            rank = (both[:, :LANES] + ahead).astype(jnp.int32)
            place = jnp.where(named, rank + target * capacity, place)
        return place

    place = jnp.zeros((rows, LANES), jnp.int32)
    if chunk == devices:
        place = ranks(0, place)
    else:
        place = lax.fori_loop(0, devices // chunk, ranks, place)
    place_ref[...] = place
    acc_ref[...] = jnp.zeros_like(acc_ref)
    group_id = iota((groups, LANES), 0)
    lane_id = iota((wide, LANES), 0)

    def spread(step, carry):
        total = None
        for u in range(4):
            row = step * 4 + u
            at = place_ref[pl.ds(row, 1), :]
            hit = group_id == at // wide
            column = (lane_id == at % wide).astype(F32).astype(BF16)
            parts = []
            for c in range(3):
                value = val_ref[c, pl.ds(row, 1), :]
                high = value.astype(BF16).astype(F32)
                low = value - high
                parts.append(
                    jnp.concatenate(
                        [jnp.where(hit, high, 0.0).astype(BF16), jnp.where(hit, low, 0.0).astype(BF16)],
                        axis=1,
                    )
                )
            left = jnp.concatenate(parts, axis=0)
            right = jnp.concatenate([column, column], axis=1)
            product = lax.dot_general(
                left, right, (((1,), (1,)), ((), ())), preferred_element_type=F32
            )
            total = product if total is None else total + product
        acc_ref[...] += total
        return carry

    lax.fori_loop(0, rows // 4, spread, 0)
    pieces = capacity // LANES
    for o in range(devices):
        for c in range(3):
            for b in range(pieces):
                m = o * pieces + b
                out_ref[o, pl.ds(c * pieces + b, 1), :] = acc_ref[
                    pl.ds(c * groups + m // 2, 1), pl.ds((m % 2) * LANES, LANES)
                ]


def wall_kernel(recv_ref, slot_ref, weight_ref, out_ref, table_ref, both_ref):
    devices, pieces = recv_ref.shape[0], recv_ref.shape[1] // 3
    groups = devices * pieces
    stencil, nodes = slot_ref.shape[0], slot_ref.shape[1]
    for c in range(3):
        for o in range(devices):
            table_ref[pl.ds(c * groups + o * pieces, pieces), :] = recv_ref[
                o, pl.ds(c * pieces, pieces), :
            ]
    high, low = split_two(table_ref[...])
    both_ref[:, :LANES] = high
    both_ref[:, LANES:] = low
    wide = 2 * LANES
    lane_id = iota((LANES, wide), 0)
    group_id = iota((groups, wide), 0)

    def pair(step, carry):
        sums = [None] * 3
        for t in range(stencil):
            slot = jnp.concatenate(
                [slot_ref[t, pl.ds(2 * step, 1), :], slot_ref[t, pl.ds(2 * step + 1, 1), :]], axis=1
            )
            weight = jnp.concatenate(
                [weight_ref[t, pl.ds(2 * step, 1), :], weight_ref[t, pl.ds(2 * step + 1, 1), :]],
                axis=1,
            )
            pick = (lane_id == slot % LANES).astype(F32).astype(BF16)
            found = jnp.dot(
                both_ref[...], jnp.concatenate([pick, pick], axis=0), preferred_element_type=F32
            )
            scaled = jnp.where(group_id == slot // LANES, weight, 0.0)
            for c in range(3):
                term = found[c * groups : (c + 1) * groups] * scaled
                sums[c] = term if sums[c] is None else sums[c] + term
        for c in range(3):
            line = jnp.sum(sums[c], axis=0, keepdims=True)
            out_ref[c, pl.ds(2 * step, 1), :] = line[:, :LANES]
            out_ref[c, pl.ds(2 * step + 1, 1), :] = line[:, LANES:]
        return carry

    lax.fori_loop(0, nodes // 2, pair, 0)


def swap_corners(corners, flip_y, flip_z):
    middle = {}
    for a, b, c in CORNERS:
        middle[a, b, c] = [
            jnp.where(flip_y, q, p) for p, q in zip(corners[a, b, c], corners[a, 1 - b, c])
        ]
    return {
        (a, b, c): [jnp.where(flip_z, q, p) for p, q in zip(middle[a, b, c], middle[a, b, 1 - c])]
        for a, b, c in CORNERS
    }


def paths():
    for order in STEP_ORDERS:
        position, path = [0, 0, 0], []
        for axis_id in order:
            position[axis_id] = 1
            path.append(tuple(position))
        yield path


def cross(p, q):
    return [p[1] * q[2] - p[2] * q[1], p[2] * q[0] - p[0] * q[2], p[0] * q[1] - p[1] * q[0]]


def add_to(table, key, vector):
    table[key] = [p + q for p, q in zip(table[key], vector)] if key in table else list(vector)


def cell_gradients(offsets, flip_y, flip_z):
    offsets = swap_corners(offsets, flip_y, flip_z)
    sign_y, sign_z = jnp.where(flip_y, -1.0, 1.0), jnp.where(flip_z, -1.0, 1.0)
    anchor = offsets[0, 0, 0]
    edges = {}
    for vertex in CORNERS[1:]:
        edge = [p - q for p, q in zip(offsets[vertex], anchor)]
        if vertex[0]:
            edge[0] = edge[0] + 1.0
        if vertex[1]:
            edge[1] = edge[1] + sign_y
        if vertex[2]:
            edge[2] = edge[2] + sign_z
        edges[vertex] = edge
    gradients, diagonal = [], {}
    for path in paths():
        one, two, three = [edges[v] for v in path]
        across = [cross(two, three), cross(three, one), cross(one, two)]
        volume = one[0] * across[0][0] + one[1] * across[0][1] + one[2] * across[0][2]
        inverse = 1.0 / volume
        grads = [[p * inverse for p in vector] for vector in across]
        gradients.append(grads)
        first = [-(grads[0][p] + grads[1][p] + grads[2][p]) for p in range(3)]
        for vertex, grad in zip([(0, 0, 0)] + path, [first] + grads):
            square = [p * p for p in grad]
            norm = square[0] + square[1] + square[2]
            add_to(diagonal, vertex, [(LAMBDA_RATIO + 1.0) * p + norm for p in square])
    return gradients, swap_corners(diagonal, flip_y, flip_z)


def cell_forces(gradients, motion, flip_y, flip_z):
    motion = swap_corners(motion, flip_y, flip_z)
    anchor = motion[0, 0, 0]
    moves = {v: [p - q for p, q in zip(motion[v], anchor)] for v in CORNERS[1:]}
    forces = {}
    for tet, path in enumerate(paths()):
        grads = [[gradients(tet, v, p) for p in range(3)] for v in range(3)]
        tensor = [
            [
                moves[path[0]][p] * grads[0][q]
                + moves[path[1]][p] * grads[1][q]
                + moves[path[2]][p] * grads[2][q]
                for q in range(3)
            ]
            for p in range(3)
        ]
        trace = LAMBDA_RATIO * (tensor[0][0] + tensor[1][1] + tensor[2][2])
        stress = [[None] * 3 for _ in range(3)]
        for p in range(3):
            stress[p][p] = tensor[p][p] + tensor[p][p] + trace
            for q in range(p):
                stress[p][q] = stress[q][p] = tensor[p][q] + tensor[q][p]
        for v in range(3):
            add_to(
                forces,
                path[v],
                [
                    stress[p][0] * grads[v][0] + stress[p][1] * grads[v][1] + stress[p][2] * grads[v][2]
                    for p in range(3)
                ],
            )
    first = None
    for vector in forces.values():
        first = vector if first is None else [p + q for p, q in zip(first, vector)]
    forces[0, 0, 0] = [-p for p in first]
    return swap_corners(forces, flip_y, flip_z)


def sweep_kernel(field_ref, wall_ref, out_ref, grad_ref, strip_grad_ref, motion_ref, force_ref, diag_ref):
    rows, depth, width = field_ref.shape[1:]
    free = width
    count_y, count_z = out_ref.shape[1:3]
    lane = iota((depth, free), 1)

    def turn(x, shift, axis):
        return pltpu.roll(x, shift % x.shape[axis], axis)

    def main_corners(low, edge):
        corners = {}
        for b in (0, 1):
            for c in (0, 1):
                near = [turn(p, -1, 0) if c else p for p in low[b]]
                corners[0, b, c] = near
                joined = [jnp.where(lane == 0, w, p) for p, w in zip(low[b], edge[b])]
                far = [turn(p, -1, 1) for p in joined]
                corners[1, b, c] = [turn(p, -1, 0) if c else p for p in far]
        return corners

    def main_assemble(parts, b):
        near = [p + turn(q, 1, 0) for p, q in zip(parts[0, b, 0], parts[0, b, 1])]
        far = [p + turn(q, 1, 0) for p, q in zip(parts[1, b, 0], parts[1, b, 1])]
        return [p + jnp.where(lane == 0, 0.0, turn(q, 1, 1)) for p, q in zip(near, far)]

    def strip_corners(near, far):
        corners = {}
        for a, column in ((0, near), (1, far)):
            for b in (0, 1):
                shifted = [turn(p, -1, 1) if b else p for p in column]
                corners[a, b, 0] = shifted
                corners[a, b, 1] = [turn(p, -1, 0) for p in shifted]
        return corners

    def strip_assemble(parts):
        low = [p + turn(q, 1, 0) for p, q in zip(parts[1, 0, 0], parts[1, 0, 1])]
        high = [p + turn(q, 1, 0) for p, q in zip(parts[1, 1, 0], parts[1, 1, 1])]
        return [p + turn(q, 1, 1) for p, q in zip(low, high)]

    def column_strip(read, source):
        total = jnp.zeros((depth, free), F32)
        for j in range(rows):
            total = jnp.where(lane == j, turn(read(j), j - source, 1), total)
        return total

    def codes(value):
        return value >= 1.5, (value == 1.0) | (value == 3.0)

    last = free - 1
    near_offset = [column_strip(lambda j: field_ref[3 + c, j], last) for c in range(3)]
    far_offset = [column_strip(lambda j: field_ref[c, j], 0) for c in range(3)]
    strip_code = column_strip(lambda j: field_ref[7, j], last)
    strip_y, strip_z = codes(strip_code)
    gradients, parts = cell_gradients(strip_corners(near_offset, far_offset), strip_y, strip_z)
    for tet in range(6):
        for v in range(3):
            for p in range(3):
                strip_grad_ref[9 * tet + 3 * v + p] = gradients[tet][v][p]
    strip_diagonal = strip_assemble(parts)
    for j in range(rows):
        for c in range(3):
            diag_ref[j, c] = jnp.where(lane == 0, turn(strip_diagonal[c], -j, 1), 0.0)

    def prepare(j, carry):
        flip_y, flip_z = codes(field_ref[6, j])
        offsets = main_corners(
            [[field_ref[c, j + b] for c in range(3)] for b in (0, 1)],
            [[field_ref[3 + c, j + b] for c in range(3)] for b in (0, 1)],
        )
        gradients, parts = cell_gradients(offsets, flip_y, flip_z)
        for tet in range(6):
            for v in range(3):
                for p in range(3):
                    grad_ref[j, 9 * tet + 3 * v + p] = gradients[tet][v][p]
        for b in (0, 1):
            for c, value in enumerate(main_assemble(parts, b)):
                diag_ref[j + b, c] = diag_ref[j + b, c] + value
        return carry

    lax.fori_loop(0, rows - 1, prepare, 0)
    for c in range(3):
        motion_ref[c] = field_ref[8 + c]
    near_wall = [column_strip(lambda j: wall_ref[c, j], last) for c in range(3)]

    for sweep in range(SWEEPS):
        far_free = [column_strip(lambda j: motion_ref[c, j], 0) for c in range(3)]
        parts = cell_forces(
            lambda tet, v, p: strip_grad_ref[9 * tet + 3 * v + p],
            strip_corners(near_wall, far_free),
            strip_y,
            strip_z,
        )
        strip_force = strip_assemble(parts)
        for j in range(sweep, rows - sweep):
            for c in range(3):
                force_ref[j, c] = jnp.where(lane == 0, turn(strip_force[c], -j, 1), 0.0)

        def push(j, carry):
            flip_y, flip_z = codes(field_ref[6, j])
            motion = main_corners(
                [[motion_ref[c, j + b] for c in range(3)] for b in (0, 1)],
                [[wall_ref[c, j + b] for c in range(3)] for b in (0, 1)],
            )
            parts = cell_forces(
                lambda tet, v, p: grad_ref[j, 9 * tet + 3 * v + p], motion, flip_y, flip_z
            )
            for b in (0, 1):
                for c, value in enumerate(main_assemble(parts, b)):
                    force_ref[j + b, c] = force_ref[j + b, c] + value
            return carry

        lax.fori_loop(sweep, rows - 1 - sweep, push, 0)
        for j in range(sweep + 1, rows - 1 - sweep):
            for c in range(3):
                motion_ref[c, j] = motion_ref[c, j] - RELAX_FACTOR * force_ref[j, c] / diag_ref[j, c]
    for c in range(3):
        for j in range(count_y):
            out_ref[c, j] = motion_ref[c, SWEEPS + j, SWEEPS : SWEEPS + count_z, :]


def call(kernel, out_shape, scratch, *operands):
    spec = pl.BlockSpec(memory_space=pltpu.VMEM)
    return pl.pallas_call(
        kernel,
        out_shape=out_shape,
        in_specs=[spec] * len(operands),
        out_specs=spec,
        scratch_shapes=scratch,
        compiler_params=pltpu.CompilerParams(vmem_limit_bytes=48 << 20),
    )(*operands)


def shards(shell_motion, owner, stencil_slot, stencil_weight, prev_motion, node_offset, cell_split):
    devices = lax.axis_size("struct") * lax.axis_size("fluid")
    own = shell_motion.shape[1]
    capacity = 2 * own // devices
    pieces = capacity // LANES
    slots = devices * capacity
    stencil, count_y, count_z, wall = stencil_slot.shape
    free = prev_motion.shape[3] - wall
    codes = cell_split[None].astype(F32)
    fields = jnp.concatenate(
        [
            node_offset[..., wall:],
            node_offset[..., :wall],
            codes[..., wall:],
            codes[..., :wall],
            prev_motion[..., wall:],
        ],
        axis=0,
    )
    fields = widen(widen(fields, "fluid", 2, SWEEPS), "struct", 1, SWEEPS)
    packed = call(
        functools.partial(pack_kernel, devices, capacity),
        jax.ShapeDtypeStruct((devices, 3 * pieces, LANES), F32),
        [
            pltpu.VMEM((own // LANES, LANES), jnp.int32),
            pltpu.VMEM((3 * slots // (2 * LANES), 2 * LANES), F32),
        ],
        owner.reshape(own // LANES, LANES),
        shell_motion.reshape(3, own // LANES, LANES),
    )
    received = lax.all_to_all(
        packed, ("struct", "fluid"), split_axis=0, concat_axis=0, tiled=True
    )
    wall_values = call(
        wall_kernel,
        jax.ShapeDtypeStruct((3, count_y * count_z, wall), F32),
        [
            pltpu.VMEM((3 * slots // LANES, LANES), F32),
            pltpu.VMEM((3 * slots // LANES, 2 * LANES), BF16),
        ],
        received,
        stencil_slot.reshape(stencil, count_y * count_z, wall),
        stencil_weight.reshape(stencil, count_y * count_z, wall),
    ).reshape(3, count_y, count_z, wall)
    walls = widen(widen(wall_values, "fluid", 2, SWEEPS), "struct", 1, SWEEPS)
    rows, depth = walls.shape[1:3]
    moved = call(
        sweep_kernel,
        jax.ShapeDtypeStruct((3, count_y, count_z, free), F32),
        [
            pltpu.VMEM((rows - 1, 54, depth, free), F32),
            pltpu.VMEM((54, depth, free), F32),
            pltpu.VMEM((3, rows, depth, free), F32),
            pltpu.VMEM((rows, 3, depth, free), F32),
            pltpu.VMEM((rows, 3, depth, free), F32),
        ],
        fields,
        walls,
    )
    return jnp.concatenate([wall_values, moved], axis=3)


def solution(mesh):
    return jax.shard_map(
        shards,
        mesh=mesh,
        in_specs=(
            P(None, ("struct", "fluid")),
            P(("struct", "fluid"), None),
            P(None, "struct", "fluid", None),
            P(None, "struct", "fluid", None),
            P(None, "struct", "fluid", None),
            P(None, "struct", "fluid", None),
            P("struct", "fluid", None),
        ),
        out_specs=P(None, "struct", "fluid", None),
        check_vma=False,
    )
```

```python
import functools

import jax
import jax.numpy as jnp
from jax import lax
from jax.experimental import pallas as pl
from jax.experimental.pallas import tpu as pltpu
from jax.sharding import PartitionSpec as P

SWEEPS = 4
LANES = 128
LAMBDA_RATIO = 1.0
RELAX_FACTOR = 0.5
STEP_ORDERS = ((0, 1, 2), (0, 2, 1), (1, 0, 2), (1, 2, 0), (2, 0, 1), (2, 1, 0))
CORNERS = tuple((a, b, c) for a in (0, 1) for b in (0, 1) for c in (0, 1))
BF16 = jnp.bfloat16
F32 = jnp.float32


def from_behind(block, axis, distance):
    count = lax.axis_size(axis)
    route = [((i - distance) % count, i) for i in range(count)]
    return lax.ppermute(block, axis, route)


def widen(block, axis, dim, depth):
    count, size = lax.axis_size(axis), block.shape[dim]
    whole = {0: block}

    def part(distance, low, high):
        key = distance % count
        if high - low < size and key != 0:
            return from_behind(lax.slice_in_dim(block, low, high, axis=dim), axis, distance)
        if key not in whole:
            whole[key] = from_behind(block, axis, distance)
        return lax.slice_in_dim(whole[key], low, high, axis=dim)

    below, above, left = [], [], depth
    distance = 1
    while left > 0:
        taken = min(left, size)
        below.insert(0, part(distance, size - taken, size))
        above.append(part(-distance, 0, taken))
        left -= taken
        distance += 1
    return jnp.concatenate(below + [block] + above, axis=dim)


def split_two(values):
    high = values.astype(BF16)
    low = (values - high.astype(F32)).astype(BF16)
    return high, low


def iota(shape, dim):
    return lax.broadcasted_iota(jnp.int32, shape, dim)


def place_kernel(devices, capacity, own_ref, place_ref):
    rows = own_ref.shape[0]
    own = own_ref[...]
    upper = (iota((LANES, LANES), 0) < iota((LANES, LANES), 1)).astype(F32)
    prefix_all = jnp.concatenate([upper, jnp.ones((LANES, LANES), F32)], axis=1).astype(BF16)
    lower = (iota((rows, rows), 1) < iota((rows, rows), 0)).astype(F32).astype(BF16)
    chunk = min(devices, 32)

    def ranks(step, place):
        for o in range(chunk):
            target = step * chunk + o
            named = own == target
            both = jnp.dot(named.astype(F32).astype(BF16), prefix_all, preferred_element_type=F32)
            ahead = jnp.dot(lower, both[:, LANES:].astype(BF16), preferred_element_type=F32)
            rank = (both[:, :LANES] + ahead).astype(jnp.int32)
            place = jnp.where(named, rank + target * capacity, place)
        return place

    place = jnp.zeros((rows, LANES), jnp.int32)
    if chunk == devices:
        place = ranks(0, place)
    else:
        place = lax.fori_loop(0, devices // chunk, ranks, place)
    place_ref[...] = place


def pack_kernel(devices, capacity, place_ref, val_ref, out_ref, acc_ref):
    rows = place_ref.shape[0]
    wide = 2 * LANES
    groups = devices * capacity // wide
    acc_ref[...] = jnp.zeros_like(acc_ref)
    group_id = iota((groups, LANES), 0)
    lane_id = iota((wide, LANES), 0)

    def spread(step, carry):
        total = None
        for u in range(4):
            row = step * 4 + u
            at = place_ref[pl.ds(row, 1), :]
            hit = group_id == at // wide
            column = (lane_id == at % wide).astype(F32).astype(BF16)
            parts = []
            for c in range(3):
                value = val_ref[c, pl.ds(row, 1), :]
                high = value.astype(BF16).astype(F32)
                low = value - high
                parts.append(
                    jnp.concatenate(
                        [jnp.where(hit, high, 0.0).astype(BF16), jnp.where(hit, low, 0.0).astype(BF16)],
                        axis=1,
                    )
                )
            left = jnp.concatenate(parts, axis=0)
            right = jnp.concatenate([column, column], axis=1)
            product = lax.dot_general(
                left, right, (((1,), (1,)), ((), ())), preferred_element_type=F32
            )
            total = product if total is None else total + product
        acc_ref[...] += total
        return carry

    lax.fori_loop(0, rows // 4, spread, 0)
    pieces = capacity // LANES
    for o in range(devices):
        for c in range(3):
            for b in range(pieces):
                m = o * pieces + b
                out_ref[o, pl.ds(c * pieces + b, 1), :] = acc_ref[
                    pl.ds(c * groups + m // 2, 1), pl.ds((m % 2) * LANES, LANES)
                ]


def wall_kernel(recv_ref, slot_ref, weight_ref, out_ref, table_ref, both_ref):
    devices, pieces = recv_ref.shape[0], recv_ref.shape[1] // 3
    groups = devices * pieces
    stencil, nodes = slot_ref.shape[0], slot_ref.shape[1]
    for c in range(3):
        for o in range(devices):
            table_ref[pl.ds(c * groups + o * pieces, pieces), :] = recv_ref[
                o, pl.ds(c * pieces, pieces), :
            ]
    high, low = split_two(table_ref[...])
    both_ref[:, :LANES] = high
    both_ref[:, LANES:] = low
    wide = 2 * LANES
    lane_id = iota((LANES, wide), 0)
    group_id = iota((groups, wide), 0)

    def pair(step, carry):
        sums = [None] * 3
        for t in range(stencil):
            slot = jnp.concatenate(
                [slot_ref[t, pl.ds(2 * step, 1), :], slot_ref[t, pl.ds(2 * step + 1, 1), :]], axis=1
            )
            weight = jnp.concatenate(
                [weight_ref[t, pl.ds(2 * step, 1), :], weight_ref[t, pl.ds(2 * step + 1, 1), :]],
                axis=1,
            )
            pick = (lane_id == slot % LANES).astype(F32).astype(BF16)
            found = jnp.dot(
                both_ref[...], jnp.concatenate([pick, pick], axis=0), preferred_element_type=F32
            )
            scaled = jnp.where(group_id == slot // LANES, weight, 0.0)
            for c in range(3):
                term = found[c * groups : (c + 1) * groups] * scaled
                sums[c] = term if sums[c] is None else sums[c] + term
        for c in range(3):
            line = jnp.sum(sums[c], axis=0, keepdims=True)
            out_ref[c, pl.ds(2 * step, 1), :] = line[:, :LANES]
            out_ref[c, pl.ds(2 * step + 1, 1), :] = line[:, LANES:]
        return carry

    lax.fori_loop(0, nodes // 2, pair, 0)


def swap_corners(corners, flip_y, flip_z):
    middle = {}
    for a, b, c in CORNERS:
        middle[a, b, c] = [
            jnp.where(flip_y, q, p) for p, q in zip(corners[a, b, c], corners[a, 1 - b, c])
        ]
    return {
        (a, b, c): [jnp.where(flip_z, q, p) for p, q in zip(middle[a, b, c], middle[a, b, 1 - c])]
        for a, b, c in CORNERS
    }


def paths():
    for order in STEP_ORDERS:
        position, path = [0, 0, 0], []
        for axis_id in order:
            position[axis_id] = 1
            path.append(tuple(position))
        yield path


def cross(p, q):
    return [p[1] * q[2] - p[2] * q[1], p[2] * q[0] - p[0] * q[2], p[0] * q[1] - p[1] * q[0]]


def add_to(table, key, vector):
    table[key] = [p + q for p, q in zip(table[key], vector)] if key in table else list(vector)


def cell_gradients(offsets, flip_y, flip_z):
    offsets = swap_corners(offsets, flip_y, flip_z)
    sign_y, sign_z = jnp.where(flip_y, -1.0, 1.0), jnp.where(flip_z, -1.0, 1.0)
    anchor = offsets[0, 0, 0]
    edges = {}
    for vertex in CORNERS[1:]:
        edge = [p - q for p, q in zip(offsets[vertex], anchor)]
        if vertex[0]:
            edge[0] = edge[0] + 1.0
        if vertex[1]:
            edge[1] = edge[1] + sign_y
        if vertex[2]:
            edge[2] = edge[2] + sign_z
        edges[vertex] = edge
    gradients, diagonal = [], {}
    for path in paths():
        one, two, three = [edges[v] for v in path]
        across = [cross(two, three), cross(three, one), cross(one, two)]
        volume = one[0] * across[0][0] + one[1] * across[0][1] + one[2] * across[0][2]
        inverse = 1.0 / volume
        grads = [[p * inverse for p in vector] for vector in across]
        gradients.append(grads)
        first = [-(grads[0][p] + grads[1][p] + grads[2][p]) for p in range(3)]
        for vertex, grad in zip([(0, 0, 0)] + path, [first] + grads):
            square = [p * p for p in grad]
            norm = square[0] + square[1] + square[2]
            add_to(diagonal, vertex, [(LAMBDA_RATIO + 1.0) * p + norm for p in square])
    return gradients, swap_corners(diagonal, flip_y, flip_z)


def cell_forces(gradients, motion, flip_y, flip_z):
    motion = swap_corners(motion, flip_y, flip_z)
    anchor = motion[0, 0, 0]
    moves = {v: [p - q for p, q in zip(motion[v], anchor)] for v in CORNERS[1:]}
    forces = {}
    for tet, path in enumerate(paths()):
        grads = [[gradients(tet, v, p) for p in range(3)] for v in range(3)]
        tensor = [
            [
                moves[path[0]][p] * grads[0][q]
                + moves[path[1]][p] * grads[1][q]
                + moves[path[2]][p] * grads[2][q]
                for q in range(3)
            ]
            for p in range(3)
        ]
        trace = LAMBDA_RATIO * (tensor[0][0] + tensor[1][1] + tensor[2][2])
        stress = [[None] * 3 for _ in range(3)]
        for p in range(3):
            stress[p][p] = tensor[p][p] + tensor[p][p] + trace
            for q in range(p):
                stress[p][q] = stress[q][p] = tensor[p][q] + tensor[q][p]
        for v in range(3):
            add_to(
                forces,
                path[v],
                [
                    stress[p][0] * grads[v][0] + stress[p][1] * grads[v][1] + stress[p][2] * grads[v][2]
                    for p in range(3)
                ],
            )
    first = None
    for vector in forces.values():
        first = vector if first is None else [p + q for p, q in zip(first, vector)]
    forces[0, 0, 0] = [-p for p in first]
    return swap_corners(forces, flip_y, flip_z)


def mesh_kernel(prepares, *refs):
    if prepares:
        field_ref, grad_ref, strip_grad_ref, diag_ref = refs
    else:
        field_ref, wall_ref, grad_ref, strip_grad_ref, diag_ref, out_ref, motion_ref, force_ref = refs
    rows, depth, free = field_ref.shape[1:]
    lane = iota((depth, free), 1)

    def turn(x, shift, axis):
        return pltpu.roll(x, shift % x.shape[axis], axis)

    def main_corners(low, edge):
        corners = {}
        for b in (0, 1):
            for c in (0, 1):
                near = [turn(p, -1, 0) if c else p for p in low[b]]
                corners[0, b, c] = near
                joined = [jnp.where(lane == 0, w, p) for p, w in zip(low[b], edge[b])]
                far = [turn(p, -1, 1) for p in joined]
                corners[1, b, c] = [turn(p, -1, 0) if c else p for p in far]
        return corners

    def main_assemble(parts, b):
        near = [p + turn(q, 1, 0) for p, q in zip(parts[0, b, 0], parts[0, b, 1])]
        far = [p + turn(q, 1, 0) for p, q in zip(parts[1, b, 0], parts[1, b, 1])]
        return [p + jnp.where(lane == 0, 0.0, turn(q, 1, 1)) for p, q in zip(near, far)]

    def strip_corners(near, far):
        corners = {}
        for a, column in ((0, near), (1, far)):
            for b in (0, 1):
                shifted = [turn(p, -1, 1) if b else p for p in column]
                corners[a, b, 0] = shifted
                corners[a, b, 1] = [turn(p, -1, 0) for p in shifted]
        return corners

    def strip_assemble(parts):
        low = [p + turn(q, 1, 0) for p, q in zip(parts[1, 0, 0], parts[1, 0, 1])]
        high = [p + turn(q, 1, 0) for p, q in zip(parts[1, 1, 0], parts[1, 1, 1])]
        return [p + turn(q, 1, 1) for p, q in zip(low, high)]

    def column_strip(read, source):
        total = jnp.zeros((depth, free), F32)
        for j in range(rows):
            total = jnp.where(lane == j, turn(read(j), j - source, 1), total)
        return total

    def codes(value):
        return value >= 1.5, (value == 1.0) | (value == 3.0)

    last = free - 1
    strip_code = column_strip(lambda j: field_ref[7, j], last)
    strip_y, strip_z = codes(strip_code)
    if prepares:
        near_offset = [column_strip(lambda j: field_ref[3 + c, j], last) for c in range(3)]
        far_offset = [column_strip(lambda j: field_ref[c, j], 0) for c in range(3)]
        gradients, parts = cell_gradients(strip_corners(near_offset, far_offset), strip_y, strip_z)
        for tet in range(6):
            for v in range(3):
                for p in range(3):
                    strip_grad_ref[9 * tet + 3 * v + p] = gradients[tet][v][p]
        strip_diagonal = strip_assemble(parts)
        for j in range(rows):
            for c in range(3):
                diag_ref[j, c] = jnp.where(lane == 0, turn(strip_diagonal[c], -j, 1), 0.0)

        def prepare(j, carry):
            flip_y, flip_z = codes(field_ref[6, j])
            offsets = main_corners(
                [[field_ref[c, j + b] for c in range(3)] for b in (0, 1)],
                [[field_ref[3 + c, j + b] for c in range(3)] for b in (0, 1)],
            )
            gradients, parts = cell_gradients(offsets, flip_y, flip_z)
            for tet in range(6):
                for v in range(3):
                    for p in range(3):
                        grad_ref[j, 9 * tet + 3 * v + p] = gradients[tet][v][p]
            for b in (0, 1):
                for c, value in enumerate(main_assemble(parts, b)):
                    diag_ref[j + b, c] = diag_ref[j + b, c] + value
            return carry

        lax.fori_loop(0, rows - 1, prepare, 0)
        return

    for c in range(3):
        motion_ref[c] = field_ref[8 + c]
    near_wall = [column_strip(lambda j: wall_ref[c, j], last) for c in range(3)]

    for sweep in range(SWEEPS):
        far_free = [column_strip(lambda j: motion_ref[c, j], 0) for c in range(3)]
        parts = cell_forces(
            lambda tet, v, p: strip_grad_ref[9 * tet + 3 * v + p],
            strip_corners(near_wall, far_free),
            strip_y,
            strip_z,
        )
        strip_force = strip_assemble(parts)
        for j in range(sweep, rows - sweep):
            for c in range(3):
                force_ref[j, c] = jnp.where(lane == 0, turn(strip_force[c], -j, 1), 0.0)

        def push(j, carry):
            flip_y, flip_z = codes(field_ref[6, j])
            motion = main_corners(
                [[motion_ref[c, j + b] for c in range(3)] for b in (0, 1)],
                [[wall_ref[c, j + b] for c in range(3)] for b in (0, 1)],
            )
            parts = cell_forces(
                lambda tet, v, p: grad_ref[j, 9 * tet + 3 * v + p], motion, flip_y, flip_z
            )
            for b in (0, 1):
                for c, value in enumerate(main_assemble(parts, b)):
                    force_ref[j + b, c] = force_ref[j + b, c] + value
            return carry

        lax.fori_loop(sweep, rows - 1 - sweep, push, 0)
        for j in range(sweep + 1, rows - 1 - sweep):
            for c in range(3):
                motion_ref[c, j] = motion_ref[c, j] - RELAX_FACTOR * force_ref[j, c] / diag_ref[j, c]
    count_y, count_z = out_ref.shape[1:3]
    for c in range(3):
        for j in range(count_y):
            out_ref[c, j] = motion_ref[c, SWEEPS + j, SWEEPS : SWEEPS + count_z, :]


def call(kernel, out_shape, scratch, flops, limit, *operands):
    spec = pl.BlockSpec(memory_space=pltpu.VMEM)
    return pl.pallas_call(
        kernel,
        out_shape=out_shape,
        in_specs=[spec] * len(operands),
        out_specs=jax.tree.map(lambda _: spec, out_shape),
        scratch_shapes=scratch,
        cost_estimate=pl.CostEstimate(flops=flops, bytes_accessed=16 << 20, transcendentals=0),
        compiler_params=pltpu.CompilerParams(vmem_limit_bytes=limit << 20),
    )(*operands)


def shards(shell_motion, owner, stencil_slot, stencil_weight, prev_motion, node_offset, cell_split):
    devices = lax.axis_size("struct") * lax.axis_size("fluid")
    own = shell_motion.shape[1]
    capacity = 2 * own // devices
    pieces = capacity // LANES
    slots = devices * capacity
    stencil, count_y, count_z, wall = stencil_slot.shape
    free = prev_motion.shape[3] - wall
    codes = cell_split[None].astype(F32)
    fields = jnp.concatenate(
        [
            node_offset[..., wall:],
            node_offset[..., :wall],
            codes[..., wall:],
            codes[..., :wall],
            prev_motion[..., wall:],
        ],
        axis=0,
    )
    fields = widen(fields, "fluid", 2, SWEEPS)
    place = call(
        functools.partial(place_kernel, devices, capacity),
        jax.ShapeDtypeStruct((own // LANES, LANES), jnp.int32),
        [],
        2 << 30,
        16,
        owner.reshape(own // LANES, LANES),
    )
    place, fields = lax.optimization_barrier((place, fields))
    fields = widen(fields, "struct", 1, SWEEPS)
    packed = call(
        functools.partial(pack_kernel, devices, capacity),
        jax.ShapeDtypeStruct((devices, 3 * pieces, LANES), F32),
        [pltpu.VMEM((3 * slots // (2 * LANES), 2 * LANES), F32)],
        4 << 30,
        16,
        place,
        shell_motion.reshape(3, own // LANES, LANES),
    )
    received = lax.all_to_all(
        packed, ("struct", "fluid"), split_axis=0, concat_axis=0, tiled=True
    )
    rows, depth = fields.shape[1:3]
    prepared = call(
        functools.partial(mesh_kernel, True),
        (
            jax.ShapeDtypeStruct((rows - 1, 54, depth, free), F32),
            jax.ShapeDtypeStruct((54, depth, free), F32),
            jax.ShapeDtypeStruct((rows, 3, depth, free), F32),
        ),
        [],
        4 << 30,
        24,
        fields,
    )
    grads, strip_grads, diag = prepared
    stencil_slot, diag = lax.optimization_barrier((stencil_slot, diag))
    prepared = (grads, strip_grads, diag)
    wall_values = call(
        wall_kernel,
        jax.ShapeDtypeStruct((3, count_y * count_z, wall), F32),
        [
            pltpu.VMEM((3 * slots // LANES, LANES), F32),
            pltpu.VMEM((3 * slots // LANES, 2 * LANES), BF16),
        ],
        4 << 30,
        16,
        received,
        stencil_slot.reshape(stencil, count_y * count_z, wall),
        stencil_weight.reshape(stencil, count_y * count_z, wall),
    ).reshape(3, count_y, count_z, wall)
    walls = widen(widen(wall_values, "fluid", 2, SWEEPS), "struct", 1, SWEEPS)
    moved = call(
        functools.partial(mesh_kernel, False),
        jax.ShapeDtypeStruct((3, count_y, count_z, free), F32),
        [pltpu.VMEM((3, rows, depth, free), F32), pltpu.VMEM((rows, 3, depth, free), F32)],
        4 << 30,
        24,
        fields,
        walls,
        *prepared,
    )
    return jnp.concatenate([wall_values, moved], axis=3)


def solution(mesh):
    return jax.shard_map(
        shards,
        mesh=mesh,
        in_specs=(
            P(None, ("struct", "fluid")),
            P(("struct", "fluid"), None),
            P(None, "struct", "fluid", None),
            P(None, "struct", "fluid", None),
            P(None, "struct", "fluid", None),
            P(None, "struct", "fluid", None),
            P("struct", "fluid", None),
        ),
        out_specs=P(None, "struct", "fluid", None),
        check_vma=False,
    )
```
